32 devices in a mesh: frag: 2 (over y), dev: 4 (over z), col: 4 (over x, core).
Axes of the slice: x: 2, y: 2, z: 4, core: 2. Of those that a mesh axis runs over, the one named last changes fastest.
Arguments:
- factor_ac: bfloat16 [3072, 32, 512], P(('frag', 'dev'), None, 'col'), parts along dimension 0, may hold values from -0.95703125 to 0.95703125
- factor_bd: bfloat16 [3072, 32, 512], P(('frag', 'col'), None, 'dev'), parts along dimension 0, may hold values from -0.95703125 to 0.95703125
- amplitudes: bfloat16 [1024, 512, 256], P(('frag', 'col'), 'dev'), parts along dimension 0, may hold values from -0.015625 to 0.015625
Outputs:
- ladder_residual: float32 [64, 32, 256], P(('frag', 'col'), 'dev'), parts along dimension 0
The draws below stay inside these ranges and needn't reach their ends.
There are 2 independent parts, one for each index of `frag`. The reference program is written for one: setup_inputs(seed, part) draws one part's arguments, and reference() takes and returns one part's arrays. A program takes and returns all parts, laid end to end along the dimension named above; each array names one. Nothing has to cross between parts.
All inputs are finite; a program needn't handle non-finite values.
Results may differ from the reference program's by a relative error of at most 0.0029.
Values may be sent and summed in bfloat16 or wider, within the bound.
No kernel may reach another device: no remote copies, remote signals or barrier semaphores. Data moves between devices by JAX's collectives and lax.ppermute only.
A program may use at most 128 MiB of HBM per device.

```python
import jax
import jax.numpy as jnp
from jax import lax

NV = 512
NAUX = 1536
AW = 32
BW = 32
NPAIR = 256


def spiked(drawn, own_key, source, target, shards_of, factor):
    owner, partner = [(jnp.arange(drawn.shape[dim]) // (drawn.shape[dim] // shards_of)).reshape([-1 if axis == dim else 1 for axis in range(drawn.ndim)]) for dim in (source, target)]
    chosen = jax.random.permutation(own_key, shards_of)[partner]
    strong = (owner == chosen) | (owner == (partner + shards_of // 2) % shards_of)
    return jnp.where(strong, factor * drawn, drawn)


def steps_of(stream_key, extent, cuts, low, top_value):
    def one(position, parts):
        draws = jax.random.uniform(jax.random.fold_in(jax.random.fold_in(stream_key, 6), position), (parts,), jnp.float32, low / len(cuts), top_value / len(cuts))
        return jnp.repeat(jnp.exp(draws), extent[position] // parts).reshape((-1,) + (1,) * (len(extent) - position - 1))

    level = one(*cuts[0])
    for cut in cuts[1:]:
        level = level * one(*cut)
    return level


def centred(own_key, shape, scale, limit, cuts=(), dtype=jnp.bfloat16):
    gain = steps_of(own_key, shape, cuts, -0.22, 0.18) if cuts else 1.0
    result = jax.random.normal(own_key, shape, jnp.float32) * scale * gain
    return jnp.minimum(jnp.maximum(result, -limit), limit).astype(dtype)


def gaussian_with(stream_key, dims, deviation, reach, cuts, heavy, held_as=jnp.bfloat16):
    drawn = deviation * jax.random.normal(stream_key, dims, jnp.float32)
    if cuts:
        drawn = drawn * steps_of(stream_key, dims, cuts, -0.22, 0.18)
    return jnp.clip(spiked(drawn, jax.random.fold_in(stream_key, 3), *heavy), -reach, reach).astype(held_as)


def setup_inputs(seed: int = 0, part: int = 0) -> dict:
    key_of = jax.random.split(jax.random.key(seed), 4)
    part_keys = jax.random.split(jax.random.fold_in(key_of[3], part), 4)
    return {
        "factor_ac": centred(part_keys[0], (NAUX, AW, NV), (NAUX ** -0.25), 0.95703125, ((0, 4), (2, 4))),
        "factor_bd": centred(part_keys[1], (NAUX, BW, NV), (NAUX ** -0.25), 0.95703125, ((0, 4), (2, 4))),
        "amplitudes": gaussian_with(part_keys[2], (NV, NV, NPAIR), (NV * NV) ** -0.5, 0.015625, ((0, 4), (1, 4)), (1, 2, 4, 2.0)),
    }


def reference(factor_ac, factor_bd, amplitudes):
    left = factor_ac.astype(jnp.float32)
    right = factor_bd.astype(jnp.float32)
    amps = amplitudes.astype(jnp.float32)
    width = NV // 8
    total = jnp.zeros((AW, BW, NPAIR), jnp.float32)
    for block in range(8):
        part_bd = right[:, :, block * width:(block + 1) * width]
        integral = jnp.einsum('qac,qbd->abdc', left, part_bd).astype(jnp.bfloat16)
        integral = lax.optimization_barrier(integral).astype(jnp.float32)
        part_amps = amps[:, block * width:(block + 1) * width, :]
        total = total + jnp.einsum('abdc,cdp->abp', integral, part_amps)
    return total
```

```python
import functools

import jax
import jax.numpy as jnp
from jax import lax
from jax.experimental import pallas as pl
from jax.experimental.pallas import tpu as pltpu
from jax.sharding import PartitionSpec as P

F32 = jnp.float32
ROWS = 8


def plain(factor_ac, factor_bd, amplitudes):
    whole_bd = lax.all_gather(factor_bd, "col", axis=0, tiled=True)
    whole_ac = lax.all_gather(factor_ac, "dev", axis=0, tiled=True)
    integral = jnp.einsum("qac,qbd->abdc", whole_ac, whole_bd, preferred_element_type=F32)
    integral = integral.astype(jnp.bfloat16)
    partial_sum = jnp.einsum("abdc,cdp->abp", integral, amplitudes, preferred_element_type=F32)
    reduced = lax.psum_scatter(partial_sum, "col", scatter_dimension=0, tiled=True)
    return lax.psum_scatter(reduced, "dev", scatter_dimension=1, tiled=True)


def block_kernel(first, z_ref, own, near, far0, far1, end0, end1, b_ref, t_ref, r_ref, out_ref, a_v, i_v):
    step = pl.program_id(0)
    z = z_ref[0]
    rows, depth = own.shape
    count = rows // ROWS
    width = b_ref.shape[2]

    def place(piece, block):
        a_v[:, pl.ds(pl.multiple_of(block * depth, 128), depth)] = piece[...]

    @pl.when(step == 0)
    def _():
        low = z < 2
        outer = (z == 0) | (z == 3)
        place(own, z)
        place(near, z + 1 - 2 * lax.rem(z, 2))
        third = jnp.where(low, 2, 1)
        fourth = jnp.where(low, 3, 0)

        @pl.when(outer)
        def _():
            place(end0, third)
            place(end1, fourth)

        @pl.when(jnp.logical_not(outer))
        def _():
            place(far0, third)
            place(far1, fourth)

    right = jnp.concatenate([b_ref[0], b_ref[1]], axis=1)
    part = jnp.dot(a_v[...], right, preferred_element_type=F32).reshape(count, ROWS, 2 * width)
    pair = jnp.concatenate([part[:, :, :width], part[:, :, width:]], axis=1)
    i_v[:, pl.ds(pl.multiple_of(2 * ROWS * step, 2 * ROWS), 2 * ROWS), :] = pair.astype(jnp.bfloat16)

    @pl.when(step == pl.num_programs(0) - 1)
    def _():
        total = jnp.zeros(out_ref.shape, F32) if first else r_ref[...]
        group = 4
        for c in range(0, count, group):
            left = jnp.concatenate([i_v[c + m] for m in range(group)], axis=1)
            amp = t_ref[c:c + group].reshape(group * width, t_ref.shape[2])
            total += jnp.dot(left, amp, preferred_element_type=F32)
        out_ref[...] = total


def block(first, z, pieces, whole_bd, amp, total):
    rows, depth = pieces[0].shape
    count = rows // ROWS
    b_count, q_count, width = whole_bd.shape
    pairs = amp.shape[2]
    fixed = lambda x: pl.BlockSpec(x.shape, lambda s, *_: (0,) * x.ndim, pipeline_mode=pl.Buffered(1))
    shape = (b_count * ROWS, pairs)
    flops = 2 * rows * q_count * b_count * width + 2 * count * width * b_count * ROWS * pairs
    return pl.pallas_call(
        functools.partial(block_kernel, first),
        grid_spec=pltpu.PrefetchScalarGridSpec(
            num_scalar_prefetch=1,
            grid=(b_count // 2,),
            in_specs=[fixed(p) for p in pieces]
            + [pl.BlockSpec((2, q_count, width), lambda s, *_: (s, 0, 0)), fixed(amp), fixed(total)],
            out_specs=pl.BlockSpec(shape, lambda s, *_: (0, 0)),
            scratch_shapes=[
                pltpu.VMEM((rows, q_count), jnp.bfloat16),
                pltpu.VMEM((count, b_count * ROWS, width), jnp.bfloat16),
            ],
        ),
        out_shape=jax.ShapeDtypeStruct(shape, F32),
        compiler_params=pltpu.CompilerParams(dimension_semantics=("arbitrary",), vmem_limit_bytes=48 * 2**20),
        cost_estimate=pl.CostEstimate(
            flops=flops, transcendentals=0, bytes_accessed=2 * (whole_bd.size + amp.size + 6 * pieces[0].size)
        ),
    )(z, *pieces, whole_bd, amp, total)


INNER = [(1, 2), (2, 1)]
TO_END = [(1, 0), (2, 3)]


def shuffled(n, mask):
    return [(i, i ^ mask) for i in range(n)]


def laddered(n_dev, n_col, factor_ac, factor_bd, amplitudes):
    depth, a_count, c_count = factor_ac.shape
    _, b_count, width = factor_bd.shape
    pairs = amplitudes.shape[2]
    dev, col = lax.axis_index("dev"), lax.axis_index("col")
    z = dev.astype(jnp.int32).reshape(1)
    chunks = a_count // ROWS
    own_rows = ROWS // n_col
    halves = 2
    span = c_count // halves
    grouped = factor_ac.reshape(depth, n_col, chunks, own_rows, c_count)

    def spread(x):
        near = lax.ppermute(x, "dev", shuffled(n_dev, 1))
        far0 = lax.ppermute(x, "dev", INNER)
        far1 = lax.ppermute(near, "dev", INNER)
        end0 = lax.ppermute(far0, "dev", TO_END)
        end1 = lax.ppermute(far1, "dev", TO_END)
        return x, near, far0, far1, end0, end1

    mine = []
    for k in range(chunks):
        turned = grouped[:, :, k].transpose(3, 1, 2, 0).reshape(c_count * ROWS, depth)
        for h in range(halves):
            mine.append(turned[h * span * ROWS:(h + 1) * span * ROWS])
    turned_bd = factor_bd.transpose(1, 0, 2)
    across = lax.ppermute(turned_bd, "col", shuffled(n_col, 2))
    beside = lax.ppermute(turned_bd, "col", shuffled(n_col, 1))
    diagonal = lax.ppermute(across, "col", shuffled(n_col, 1))
    whole_bd = jnp.zeros((b_count, depth * n_col, width), factor_bd.dtype)
    for mask, piece in enumerate((turned_bd, beside, across, diagonal)):
        whole_bd = lax.dynamic_update_slice(whole_bd, piece, (0, (col ^ mask) * depth, 0))

    def reduced(total):
        x = total.reshape(b_count, n_col // 2, 2, own_rows, pairs)
        core = col % 2
        keep = lax.dynamic_index_in_dim(x, core, 2, keepdims=False)
        give = lax.dynamic_index_in_dim(x, 1 - core, 2, keepdims=False)
        x = keep + lax.ppermute(give, "col", shuffled(n_col, 1))
        chip = col // 2
        keep = lax.dynamic_index_in_dim(x, chip, 1, keepdims=False)
        give = lax.dynamic_index_in_dim(x, 1 - chip, 1, keepdims=False)
        x = keep + lax.ppermute(give, "col", shuffled(n_col, 2))
        x = x.reshape(n_dev, b_count // n_dev, own_rows, pairs)
        out = lax.dynamic_index_in_dim(x, dev, 0, keepdims=False)
        for turn in range(1, n_dev):
            give = lax.dynamic_index_in_dim(x, (dev + turn) % n_dev, 0, keepdims=False)
            out = out + lax.ppermute(give, "dev", [(i, (i + turn) % n_dev) for i in range(n_dev)])
        return out

    results = []
    for k in range(chunks):
        total = jnp.zeros((b_count * ROWS, pairs), F32)
        for h in range(halves):
            pieces = spread(mine[k * halves + h])
            amp = amplitudes[h * span:(h + 1) * span]
            total = block(h == 0, z, pieces, whole_bd, amp, total)
        results.append(reduced(total))
    out = jnp.stack(results, axis=0)
    return out.transpose(0, 2, 1, 3).reshape(chunks * own_rows, b_count // n_dev, pairs)


def solution(mesh):
    n_dev, n_col = mesh.shape["dev"], mesh.shape["col"]
    placed = (
        P(("frag", "dev"), None, "col"),
        P(("frag", "col"), None, "dev"),
        P(("frag", "col"), "dev", None),
    )

    def local(factor_ac, factor_bd, amplitudes):
        depth, a_count, c_count = factor_ac.shape
        width = factor_bd.shape[2]
        fits = n_dev == 4 and n_col == 4 and width == 128 and depth % 128 == 0
        fits = fits and a_count == ROWS * n_col and c_count % 8 == 0
        if fits:
            return laddered(n_dev, n_col, factor_ac, factor_bd, amplitudes)
        return plain(factor_ac, factor_bd, amplitudes)

    return jax.shard_map(
        local,
        mesh=mesh,
        in_specs=placed,
        out_specs=P(("frag", "col"), "dev", None),
        check_vma=False,
    )
```

```python
import functools

import jax
import jax.numpy as jnp
from jax import lax
from jax.experimental import pallas as pl
from jax.experimental.pallas import tpu as pltpu
from jax.sharding import PartitionSpec as P


F32 = jnp.float32
ROWS = 8
WIDE = 4


def plain(factor_ac, factor_bd, amplitudes):
    whole_bd = lax.all_gather(factor_bd, "col", axis=0, tiled=True)
    whole_ac = lax.all_gather(factor_ac, "dev", axis=0, tiled=True)
    integral = jnp.einsum("qac,qbd->abdc", whole_ac, whole_bd, preferred_element_type=F32)
    integral = integral.astype(jnp.bfloat16)
    partial_sum = jnp.einsum("abdc,cdp->abp", integral, amplitudes, preferred_element_type=F32)
    reduced = lax.psum_scatter(partial_sum, "col", scatter_dimension=0, tiled=True)
    return lax.psum_scatter(reduced, "dev", scatter_dimension=1, tiled=True)


def block_kernel(first, starts, rows, c_start, where, own, near, far0, far1, end0, end1,
                 b0, b1, b2, b3, t_ref, r_ref, out_ref, a_v, b_v, t_v, i_v, a_sem, b_sem, t_sem):
    depth = own.shape[1]
    count = rows // ROWS
    b_count, _, width = b0.shape
    steps = b_count // WIDE
    sources = (own, near, far0, far1, end0, end1)

    def a_copy(index, slot):
        source = sources[index].at[pl.ds(starts[index], rows), :]
        column = pl.ds(pl.multiple_of(where[slot] * depth, 128), depth)
        return pltpu.make_async_copy(source, a_v.at[:, column], a_sem.at[slot])

    def b_copy(step, slot):
        span = pl.ds(step * WIDE, WIDE)
        deep = pl.ds(pl.multiple_of(where[4 + slot] * depth, 128), depth)
        return pltpu.make_async_copy((b0, b1, b2, b3)[slot].at[span], b_v.at[span, deep, :], b_sem.at[step, slot])

    t_copy = pltpu.make_async_copy(t_ref.at[pl.ds(c_start, count)], t_v, t_sem)
    a_copy(0, 0).start()
    a_copy(1, 1).start()

    @pl.when(where[8] == 1)
    def _():
        a_copy(4, 2).start()
        a_copy(5, 3).start()

    @pl.when(where[8] == 0)
    def _():
        a_copy(2, 2).start()
        a_copy(3, 3).start()

    for slot in range(4):
        b_copy(0, slot).start()

    def begin(step, carry):
        for slot in range(4):
            b_copy(step, slot).start()
        return carry

    lax.fori_loop(1, steps, begin, 0)
    t_copy.start()
    for slot in range(4):
        a_copy(slot, slot).wait()

    def contract(step, carry):
        for slot in range(4):
            b_copy(step, slot).wait()
        right = jnp.concatenate([b_v[step * WIDE + m] for m in range(WIDE)], axis=1)
        part = jnp.dot(a_v[...], right, preferred_element_type=F32).reshape(count, ROWS, WIDE * width)
        tall = jnp.concatenate([part[:, :, m * width:(m + 1) * width] for m in range(WIDE)], axis=1)
        i_v[:, pl.ds(pl.multiple_of(WIDE * ROWS * step, WIDE * ROWS), WIDE * ROWS), :] = tall.astype(jnp.bfloat16)
        return carry

    lax.fori_loop(0, steps, contract, 0)
    t_copy.wait()
    group = 4
    out_ref[...] = jnp.zeros(out_ref.shape, F32) if first else r_ref[...]

    def absorb(g, carry):
        c = g * group
        left = jnp.concatenate([i_v[c + m] for m in range(group)], axis=1)
        amp = t_v[pl.ds(c, group)].reshape(group * width, t_v.shape[2])
        out_ref[...] += jnp.dot(left, amp, preferred_element_type=F32)
        return carry

    lax.fori_loop(0, count // group, absorb, 0, unroll=2)


def block(first, where, pieces, starts, rows, quarters, amplitudes, c_start, total):
    depth = pieces[0].shape[1]
    count = rows // ROWS
    b_count, _, width = quarters[0].shape
    pairs = amplitudes.shape[2]
    q_count = depth * 4
    shape = (b_count * ROWS, pairs)
    flops = 2 * rows * q_count * b_count * width + 2 * count * width * b_count * ROWS * pairs
    anywhere = pl.BlockSpec(memory_space=pl.ANY)
    inside = pl.BlockSpec(memory_space=pltpu.VMEM)
    return pl.pallas_call(
        functools.partial(block_kernel, first, starts, rows, c_start),
        in_specs=[pl.BlockSpec(memory_space=pltpu.SMEM)] + [anywhere] * 11 + [inside],
        out_specs=inside,
        scratch_shapes=[
            pltpu.VMEM((rows, q_count), jnp.bfloat16),
            pltpu.VMEM((b_count, q_count, width), jnp.bfloat16),
            pltpu.VMEM((count, width, pairs), jnp.bfloat16),
            pltpu.VMEM((count, b_count * ROWS, width), jnp.bfloat16),
            pltpu.SemaphoreType.DMA((4,)),
            pltpu.SemaphoreType.DMA((b_count // WIDE, 4)),
            pltpu.SemaphoreType.DMA,
        ],
        out_shape=jax.ShapeDtypeStruct(shape, F32),
        compiler_params=pltpu.CompilerParams(vmem_limit_bytes=66977792),
        cost_estimate=pl.CostEstimate(
            flops=flops,
            transcendentals=0,
            bytes_accessed=2 * (b_count * q_count * width + count * width * pairs + rows * q_count),
        ),
    )(where, *pieces, *quarters, amplitudes, total)


INNER = [(1, 2), (2, 1)]
TO_END = [(1, 0), (2, 3)]


def shuffled(n, mask):
    return [(i, i ^ mask) for i in range(n)]


def laddered(n_dev, n_col, factor_ac, factor_bd, amplitudes):
    depth, a_count, c_count = factor_ac.shape
    _, b_count, _ = factor_bd.shape
    pairs = amplitudes.shape[2]
    dev, col = lax.axis_index("dev").astype(jnp.int32), lax.axis_index("col").astype(jnp.int32)
    low = dev < 2
    outer = (dev == 0) | (dev == 3)
    where = [dev, dev ^ 1, jnp.where(low, 2, 1), jnp.where(low, 3, 0), col, col ^ 1, col ^ 2, col ^ 3, outer]
    where = jnp.stack([x.astype(jnp.int32) for x in where])
    groups = a_count // ROWS
    halves = 2
    each = groups // halves
    tall = c_count * ROWS
    mid = c_count // 2

    def turned(h):
        x = factor_ac[:, h * each * ROWS:(h + 1) * each * ROWS].reshape(depth, each, ROWS, c_count)
        return x.transpose(1, 3, 2, 0).reshape(each * tall, depth)

    own = [turned(h) for h in range(halves)]
    turned_bd = factor_bd.transpose(1, 0, 2)
    near = [lax.ppermute(x, "dev", shuffled(n_dev, 1)) for x in own]
    far0 = [lax.ppermute(x, "dev", INNER) for x in own]
    far1 = [lax.ppermute(x, "dev", INNER) for x in near]
    end0 = [lax.ppermute(x, "dev", TO_END) for x in far0]
    across = lax.ppermute(turned_bd, "col", shuffled(n_col, 2))
    beside = lax.ppermute(turned_bd, "col", shuffled(n_col, 1))
    diagonal = lax.ppermute(across, "col", shuffled(n_col, 1))
    quarters = (turned_bd, beside, across, diagonal)

    def reduced(group, total):
        with_core = [(i, i ^ 1) for i in range(n_col) if i % 2 != group % 2]
        total = total + lax.ppermute(total, "col", with_core)
        total = total + lax.ppermute(total, "col", [(group ^ 2, group)])
        x = total.reshape(n_dev, b_count // n_dev * ROWS, pairs)
        out = lax.dynamic_index_in_dim(x, dev, 0, keepdims=False)
        for mask in range(1, n_dev):
            give = lax.dynamic_index_in_dim(x, dev ^ mask, 0, keepdims=False)
            pattern = [(i * n_col + group, (i ^ mask) * n_col + group) for i in range(n_dev)]
            out = out + lax.ppermute(give, ("dev", "col"), pattern)
        return out

    plan = [[(g, [(0, c_count)]) for g in range(each)] for _ in range(halves)]
    plan[-1][-1] = (each - 1, [(0, mid), (mid, c_count)])
    totals = []
    for h in range(halves):
        for g, spans in plan[h]:
            total = jnp.zeros((b_count * ROWS, pairs), F32)
            for c0, c1 in spans:
                start, rows = g * tall + c0 * ROWS, (c1 - c0) * ROWS
                end1 = lax.ppermute(far1[h][start:start + rows], "dev", TO_END)
                pieces = (own[h], near[h], far0[h], far1[h], end0[h], end1)
                starts = (start,) * 5 + (0,)
                total = block(c0 == 0, where, pieces, starts, rows, quarters, amplitudes, c0, total)
            totals.append(total)
    out = jnp.zeros((b_count // n_dev * ROWS, pairs), F32)
    previous = None
    for group, total in enumerate(totals):
        if previous is not None:
            total, previous = lax.optimization_barrier((total, previous))
        previous = reduced(group, total)
        out = jnp.where(col == group, previous, out)
    return out.reshape(b_count // n_dev, ROWS, pairs).transpose(1, 0, 2)


def solution(mesh):
    n_dev, n_col = mesh.shape["dev"], mesh.shape["col"]
    placed = (
        P(("frag", "dev"), None, "col"),
        P(("frag", "col"), None, "dev"),
        P(("frag", "col"), "dev", None),
    )

    def local(factor_ac, factor_bd, amplitudes):
        depth, a_count, c_count = factor_ac.shape
        _, b_count, width = factor_bd.shape
        fits = n_dev == 4 and n_col == 4 and width == 128 and depth % 128 == 0
        fits = fits and a_count == ROWS * n_col and b_count % 8 == 0 and c_count % 8 == 0
        if fits:
            return laddered(n_dev, n_col, factor_ac, factor_bd, amplitudes)
        return plain(factor_ac, factor_bd, amplitudes)

    return jax.shard_map(
        local,
        mesh=mesh,
        in_specs=placed,
        out_specs=P(("frag", "col"), "dev", None),
        check_vma=False,
    )
```

```python
import functools

import jax
import jax.numpy as jnp
from jax import lax
from jax.experimental import pallas as pl
from jax.experimental.pallas import tpu as pltpu
from jax.sharding import PartitionSpec as P


F32 = jnp.float32
ROWS = 8
WIDE = 4


def plain(factor_ac, factor_bd, amplitudes):
    whole_bd = lax.all_gather(factor_bd, "col", axis=0, tiled=True)
    whole_ac = lax.all_gather(factor_ac, "dev", axis=0, tiled=True)
    integral = jnp.einsum("qac,qbd->abdc", whole_ac, whole_bd, preferred_element_type=F32)
    integral = integral.astype(jnp.bfloat16)
    partial_sum = jnp.einsum("abdc,cdp->abp", integral, amplitudes, preferred_element_type=F32)
    reduced = lax.psum_scatter(partial_sum, "col", scatter_dimension=0, tiled=True)
    return lax.psum_scatter(reduced, "dev", scatter_dimension=1, tiled=True)


def block_kernel(first, starts, rows, c_start, where, own, near, far0, far1, end0, end1,
                 b0, b1, b2, b3, t_ref, r_ref, out_ref, a_v, b_v, t_v, i_v, a_sem, b_sem, t_sem):
    depth = own.shape[1]
    count = rows // ROWS
    b_count, _, width = b0.shape
    steps = b_count // WIDE
    sources = (own, near, far0, far1, end0, end1)

    def a_copy(index, slot):
        source = sources[index].at[pl.ds(starts[index], rows), :]
        column = pl.ds(pl.multiple_of(where[slot] * depth, 128), depth)
        return pltpu.make_async_copy(source, a_v.at[:, column], a_sem.at[slot])

    def b_copy(step, slot):
        span = pl.ds(step * WIDE, WIDE)
        deep = pl.ds(pl.multiple_of(where[4 + slot] * depth, 128), depth)
        return pltpu.make_async_copy((b0, b1, b2, b3)[slot].at[span], b_v.at[span, deep, :], b_sem.at[step, slot])

    t_copy = pltpu.make_async_copy(t_ref.at[pl.ds(c_start, count)], t_v, t_sem)
    a_copy(0, 0).start()
    a_copy(1, 1).start()

    @pl.when(where[8] == 1)
    def _():
        a_copy(4, 2).start()
        a_copy(5, 3).start()

    @pl.when(where[8] == 0)
    def _():
        a_copy(2, 2).start()
        a_copy(3, 3).start()

    for slot in range(4):
        b_copy(0, slot).start()

    def begin(step, carry):
        for slot in range(4):
            b_copy(step, slot).start()
        return carry

    lax.fori_loop(1, steps, begin, 0)
    t_copy.start()
    for slot in range(4):
        a_copy(slot, slot).wait()

    def contract(step, carry):
        for slot in range(4):
            b_copy(step, slot).wait()
        right = jnp.concatenate([b_v[step * WIDE + m] for m in range(WIDE)], axis=1)
        part = jnp.dot(a_v[...], right, preferred_element_type=F32).reshape(count, ROWS, WIDE * width)
        tall = jnp.concatenate([part[:, :, m * width:(m + 1) * width] for m in range(WIDE)], axis=1)
        i_v[:, pl.ds(pl.multiple_of(WIDE * ROWS * step, WIDE * ROWS), WIDE * ROWS), :] = tall.astype(jnp.bfloat16)
        return carry

    lax.fori_loop(0, steps, contract, 0)
    t_copy.wait()
    group = 4
    out_ref[...] = jnp.zeros(out_ref.shape, F32) if first else r_ref[...]

    def absorb(g, carry):
        c = g * group
        left = jnp.concatenate([i_v[c + m] for m in range(group)], axis=1)
        amp = t_v[pl.ds(c, group)].reshape(group * width, t_v.shape[2])
        out_ref[...] += jnp.dot(left, amp, preferred_element_type=F32)
        return carry

    lax.fori_loop(0, count // group, absorb, 0, unroll=2)


def block(first, where, pieces, starts, rows, quarters, amplitudes, c_start, total):
    depth = pieces[0].shape[1]
    count = rows // ROWS
    b_count, _, width = quarters[0].shape
    pairs = amplitudes.shape[2]
    q_count = depth * 4
    shape = (b_count * ROWS, pairs)
    flops = 2 * rows * q_count * b_count * width + 2 * count * width * b_count * ROWS * pairs
    anywhere = pl.BlockSpec(memory_space=pl.ANY)
    inside = pl.BlockSpec(memory_space=pltpu.VMEM)
    return pl.pallas_call(
        functools.partial(block_kernel, first, starts, rows, c_start),
        in_specs=[pl.BlockSpec(memory_space=pltpu.SMEM)] + [anywhere] * 11 + [inside],
        out_specs=inside,
        scratch_shapes=[
            pltpu.VMEM((rows, q_count), jnp.bfloat16),
            pltpu.VMEM((b_count, q_count, width), jnp.bfloat16),
            pltpu.VMEM((count, width, pairs), jnp.bfloat16),
            pltpu.VMEM((count, b_count * ROWS, width), jnp.bfloat16),
            pltpu.SemaphoreType.DMA((4,)),
            pltpu.SemaphoreType.DMA((b_count // WIDE, 4)),
            pltpu.SemaphoreType.DMA,
        ],
        out_shape=jax.ShapeDtypeStruct(shape, F32),
        compiler_params=pltpu.CompilerParams(vmem_limit_bytes=66977792),
        cost_estimate=pl.CostEstimate(
            flops=flops,
            transcendentals=0,
            bytes_accessed=2 * (b_count * q_count * width + count * width * pairs + rows * q_count),
        ),
    )(where, *pieces, *quarters, amplitudes, total)


INNER = [(1, 2), (2, 1)]
TO_END = [(1, 0), (2, 3)]


def shuffled(n, mask):
    return [(i, i ^ mask) for i in range(n)]


def laddered(n_dev, n_col, factor_ac, factor_bd, amplitudes):
    depth, a_count, c_count = factor_ac.shape
    _, b_count, _ = factor_bd.shape
    pairs = amplitudes.shape[2]
    dev, col = lax.axis_index("dev").astype(jnp.int32), lax.axis_index("col").astype(jnp.int32)
    low = dev < 2
    outer = (dev == 0) | (dev == 3)
    where = [dev, dev ^ 1, jnp.where(low, 2, 1), jnp.where(low, 3, 0), col, col ^ 1, col ^ 2, col ^ 3, outer]
    where = jnp.stack([x.astype(jnp.int32) for x in where])
    groups = a_count // ROWS
    mid = c_count // 2
    spans = [[(0, c_count)]] * (groups - 1) + [[(0, mid), (mid, c_count)]]

    def turned(g):
        return factor_ac[:, g * ROWS:(g + 1) * ROWS].transpose(2, 1, 0).reshape(c_count * ROWS, depth)

    def ends(g, x):
        parts = [x[c0 * ROWS:c1 * ROWS] for c0, c1 in spans[g]] if len(spans[g]) > 1 else [x]
        return [lax.ppermute(part, "dev", TO_END) for part in parts]

    own = [turned(g) for g in range(groups)]
    turned_bd = factor_bd.transpose(1, 0, 2)
    near = [lax.ppermute(x, "dev", shuffled(n_dev, 1)) for x in own]
    far0 = [lax.ppermute(x, "dev", INNER) for x in own]
    far1 = [lax.ppermute(x, "dev", INNER) for x in near]
    end0 = [ends(g, x) for g, x in enumerate(far0)]
    end1 = [ends(g, x) for g, x in enumerate(far1)]
    across = lax.ppermute(turned_bd, "col", shuffled(n_col, 2))
    beside = lax.ppermute(turned_bd, "col", shuffled(n_col, 1))
    diagonal = lax.ppermute(across, "col", shuffled(n_col, 1))
    quarters = (turned_bd, beside, across, diagonal)

    def scattered(total, columns):
        x = total.reshape(n_dev, b_count // n_dev * ROWS, pairs)
        out = lax.dynamic_index_in_dim(x, dev, 0, keepdims=False)
        for mask in range(1, n_dev):
            give = lax.dynamic_index_in_dim(x, dev ^ mask, 0, keepdims=False)
            pattern = [(i * n_col + j, (i ^ mask) * n_col + j) for i in range(n_dev) for j in columns]
            out = out + lax.ppermute(give, ("dev", "col"), pattern)
        return out

    def reduced(group, total):
        with_core = [(i, i ^ 1) for i in range(n_col) if i % 2 != group % 2]
        early = total + lax.ppermute(total, "col", with_core)
        total = early + lax.ppermute(early, "col", [(group ^ 2, group)])
        return scattered(total, (group,)), early

    def reduced_pair(even, odd):
        core = col % 2
        keep, give = jnp.where(core == 0, even, odd), jnp.where(core == 0, odd, even)
        total = keep + lax.ppermute(give, "col", shuffled(n_col, 1))
        total = total + lax.ppermute(total, "col", [(2, 0), (3, 1)])
        return scattered(total, (0, 1))

    totals = []
    for g in range(groups):
        total = jnp.zeros((b_count * ROWS, pairs), F32)
        for i, (c0, c1) in enumerate(spans[g]):
            pieces = (own[g], near[g], far0[g], far1[g], end0[g][i], end1[g][i])
            starts = (c0 * ROWS,) * 4 + (0, 0)
            total = block(i == 0, where, pieces, starts, (c1 - c0) * ROWS, quarters, amplitudes, c0, total)
        totals.append(total)
    out = reduced_pair(totals[0], totals[1])
    total, out = lax.optimization_barrier((totals[2], out))
    third, early = reduced(2, total)
    total, _ = lax.optimization_barrier((totals[3], early))
    fourth, _ = reduced(3, total)
    out = jnp.where(col == 2, third, jnp.where(col == 3, fourth, out))
    return out.reshape(b_count // n_dev, ROWS, pairs).transpose(1, 0, 2)


def solution(mesh):
    n_dev, n_col = mesh.shape["dev"], mesh.shape["col"]
    placed = (
        P(("frag", "dev"), None, "col"),
        P(("frag", "col"), None, "dev"),
        P(("frag", "col"), "dev", None),
    )

    def local(factor_ac, factor_bd, amplitudes):
        depth, a_count, c_count = factor_ac.shape
        _, b_count, width = factor_bd.shape
        fits = n_dev == 4 and n_col == 4 and width == 128 and depth % 128 == 0
        fits = fits and a_count == ROWS * n_col and b_count % 8 == 0 and c_count % 8 == 0
        if fits:
            return laddered(n_dev, n_col, factor_ac, factor_bd, amplitudes)
        return plain(factor_ac, factor_bd, amplitudes)

    return jax.shard_map(
        local,
        mesh=mesh,
        in_specs=placed,
        out_specs=P(("frag", "col"), "dev", None),
        check_vma=False,
    )
```

```python
import functools

import jax
import jax.numpy as jnp
from jax import lax
from jax.experimental import pallas as pl
from jax.experimental.pallas import tpu as pltpu
from jax.sharding import PartitionSpec as P


F32 = jnp.float32
ROWS = 8
WIDE = 4


def plain(factor_ac, factor_bd, amplitudes):
    whole_bd = lax.all_gather(factor_bd, "col", axis=0, tiled=True)
    whole_ac = lax.all_gather(factor_ac, "dev", axis=0, tiled=True)
    integral = jnp.einsum("qac,qbd->abdc", whole_ac, whole_bd, preferred_element_type=F32)
    integral = integral.astype(jnp.bfloat16)
    partial_sum = jnp.einsum("abdc,cdp->abp", integral, amplitudes, preferred_element_type=F32)
    reduced = lax.psum_scatter(partial_sum, "col", scatter_dimension=0, tiled=True)
    return lax.psum_scatter(reduced, "dev", scatter_dimension=1, tiled=True)


def block_kernel(first, starts, rows, c_start, where, own, near, far0, far1, end0, end1,
                 b0, b1, b2, b3, t_ref, r_ref, out_ref, a_v, b_v, t_v, i_v, a_sem, b_sem, t_sem):
    depth = own.shape[1]
    count = rows // ROWS
    b_count, _, width = b0.shape
    steps = b_count // WIDE
    sources = (own, near, far0, far1, end0, end1)

    def a_copy(index, slot):
        source = sources[index].at[pl.ds(starts[index], rows), :]
        column = pl.ds(pl.multiple_of(where[slot] * depth, 128), depth)
        return pltpu.make_async_copy(source, a_v.at[:, column], a_sem.at[slot])

    def b_copy(step, slot):
        span = pl.ds(step * WIDE, WIDE)
        deep = pl.ds(pl.multiple_of(where[4 + slot] * depth, 128), depth)
        return pltpu.make_async_copy((b0, b1, b2, b3)[slot].at[span], b_v.at[span, deep, :], b_sem.at[step, slot])

    t_copy = pltpu.make_async_copy(t_ref.at[pl.ds(c_start, count)], t_v, t_sem)
    a_copy(0, 0).start()
    a_copy(1, 1).start()

    @pl.when(where[8] == 1)
    def _():
        a_copy(4, 2).start()
        a_copy(5, 3).start()

    @pl.when(where[8] == 0)
    def _():
        a_copy(2, 2).start()
        a_copy(3, 3).start()

    for slot in range(4):
        b_copy(0, slot).start()

    def begin(step, carry):
        for slot in range(4):
            b_copy(step, slot).start()
        return carry

    lax.fori_loop(1, steps, begin, 0)
    t_copy.start()
    for slot in range(4):
        a_copy(slot, slot).wait()

    def contract(step, carry):
        for slot in range(4):
            b_copy(step, slot).wait()
        right = jnp.concatenate([b_v[step * WIDE + m] for m in range(WIDE)], axis=1)
        part = jnp.dot(a_v[...], right, preferred_element_type=F32).reshape(count, ROWS, WIDE * width)
        tall = jnp.concatenate([part[:, :, m * width:(m + 1) * width] for m in range(WIDE)], axis=1)
        i_v[:, pl.ds(pl.multiple_of(WIDE * ROWS * step, WIDE * ROWS), WIDE * ROWS), :] = tall.astype(jnp.bfloat16)
        return carry

    lax.fori_loop(0, steps, contract, 0)
    t_copy.wait()
    group = 8
    total = jnp.zeros(out_ref.shape, F32) if first else r_ref[...]
    for c in range(0, count, group):
        left = jnp.concatenate([i_v[c + m] for m in range(group)], axis=1)
        amp = t_v[c:c + group].reshape(group * width, t_v.shape[2])
        total += jnp.dot(left, amp, preferred_element_type=F32)
    out_ref[...] = total


def block(first, where, pieces, starts, rows, quarters, amplitudes, c_start, total):
    depth = pieces[0].shape[1]
    count = rows // ROWS
    b_count, _, width = quarters[0].shape
    pairs = amplitudes.shape[2]
    q_count = depth * 4
    shape = (b_count * ROWS, pairs)
    flops = 2 * rows * q_count * b_count * width + 2 * count * width * b_count * ROWS * pairs
    anywhere = pl.BlockSpec(memory_space=pl.ANY)
    inside = pl.BlockSpec(memory_space=pltpu.VMEM)
    return pl.pallas_call(
        functools.partial(block_kernel, first, starts, rows, c_start),
        in_specs=[pl.BlockSpec(memory_space=pltpu.SMEM)] + [anywhere] * 11 + [inside],
        out_specs=inside,
        scratch_shapes=[
            pltpu.VMEM((rows, q_count), jnp.bfloat16),
            pltpu.VMEM((b_count, q_count, width), jnp.bfloat16),
            pltpu.VMEM((count, width, pairs), jnp.bfloat16),
            pltpu.VMEM((count, b_count * ROWS, width), jnp.bfloat16),
            pltpu.SemaphoreType.DMA((4,)),
            pltpu.SemaphoreType.DMA((b_count // WIDE, 4)),
            pltpu.SemaphoreType.DMA,
        ],
        out_shape=jax.ShapeDtypeStruct(shape, F32),
        compiler_params=pltpu.CompilerParams(vmem_limit_bytes=66977792),
        cost_estimate=pl.CostEstimate(
            flops=flops,
            transcendentals=0,
            bytes_accessed=2 * (b_count * q_count * width + count * width * pairs + rows * q_count),
        ),
    )(where, *pieces, *quarters, amplitudes, total)


INNER = [(1, 2), (2, 1)]
TO_END = [(1, 0), (2, 3)]


def shuffled(n, mask):
    return [(i, i ^ mask) for i in range(n)]


def laddered(n_dev, n_col, factor_ac, factor_bd, amplitudes):
    depth, a_count, c_count = factor_ac.shape
    _, b_count, _ = factor_bd.shape
    pairs = amplitudes.shape[2]
    dev, col = lax.axis_index("dev").astype(jnp.int32), lax.axis_index("col").astype(jnp.int32)
    low = dev < 2
    outer = (dev == 0) | (dev == 3)
    where = [dev, dev ^ 1, jnp.where(low, 2, 1), jnp.where(low, 3, 0), col, col ^ 1, col ^ 2, col ^ 3, outer]
    where = jnp.stack([x.astype(jnp.int32) for x in where])
    groups = a_count // ROWS
    mid = c_count // 2
    spans = [[(0, c_count)]] * (groups - 1) + [[(0, mid), (mid, c_count)]]

    def turned(g):
        return factor_ac[:, g * ROWS:(g + 1) * ROWS].transpose(2, 1, 0).reshape(c_count * ROWS, depth)

    def ends(g, x):
        parts = [x[c0 * ROWS:c1 * ROWS] for c0, c1 in spans[g]] if len(spans[g]) > 1 else [x]
        return [lax.ppermute(part, "dev", TO_END) for part in parts]

    own = [turned(g) for g in range(groups)]
    turned_bd = factor_bd.transpose(1, 0, 2)
    near = [lax.ppermute(x, "dev", shuffled(n_dev, 1)) for x in own]
    far0 = [lax.ppermute(x, "dev", INNER) for x in own]
    far1 = [lax.ppermute(x, "dev", INNER) for x in near]
    across = lax.ppermute(turned_bd, "col", shuffled(n_col, 2))
    beside = lax.ppermute(turned_bd, "col", shuffled(n_col, 1))
    diagonal = lax.ppermute(across, "col", shuffled(n_col, 1))
    quarters = (turned_bd, beside, across, diagonal)

    def to_owner(group, total):
        with_core = [(i, i ^ 1) for i in range(n_col) if i % 2 != group % 2]
        early = total + lax.ppermute(total, "col", with_core)
        return early + lax.ppermute(early, "col", [(group ^ 2, group)]), early

    def to_owners(even, odd):
        core = col % 2
        keep, give = jnp.where(core == 0, even, odd), jnp.where(core == 0, odd, even)
        early = keep + lax.ppermute(give, "col", shuffled(n_col, 1))
        return early + lax.ppermute(early, "col", [(2, 0), (3, 1)]), early

    totals = []
    for g in range(groups):
        total = jnp.zeros((b_count * ROWS, pairs), F32)
        third, fourth = far0[g], far1[g]
        if len(spans[g]) > 1:
            third, fourth, totals[1] = lax.optimization_barrier((third, fourth, totals[1]))
        end0, end1 = ends(g, third), ends(g, fourth)
        for i, (c0, c1) in enumerate(spans[g]):
            pieces = (own[g], near[g], third, fourth, end0[i], end1[i])
            starts = (c0 * ROWS,) * 4 + (0, 0)
            total = block(i == 0, where, pieces, starts, (c1 - c0) * ROWS, quarters, amplitudes, c0, total)
        totals.append(total)
    both, early = to_owners(totals[0], totals[1])
    total, _ = lax.optimization_barrier((totals[2], early))
    third, early = to_owner(2, total)
    total, _ = lax.optimization_barrier((totals[3], early))
    fourth, _ = to_owner(3, total)
    mine = jnp.where(col == 3, fourth, jnp.where(col == 2, third, both))
    mine = mine.reshape(n_dev, b_count // n_dev * ROWS, pairs)
    out = lax.dynamic_index_in_dim(mine, dev, 0, keepdims=False)
    for mask in range(1, n_dev):
        give = lax.dynamic_index_in_dim(mine, dev ^ mask, 0, keepdims=False)
        out = out + lax.ppermute(give, "dev", shuffled(n_dev, mask))
    return out.reshape(b_count // n_dev, ROWS, pairs).transpose(1, 0, 2)


def solution(mesh):
    n_dev, n_col = mesh.shape["dev"], mesh.shape["col"]
    placed = (
        P(("frag", "dev"), None, "col"),
        P(("frag", "col"), None, "dev"),
        P(("frag", "col"), "dev", None),
    )

    def local(factor_ac, factor_bd, amplitudes):
        depth, a_count, c_count = factor_ac.shape
        _, b_count, width = factor_bd.shape
        fits = n_dev == 4 and n_col == 4 and width == 128 and depth % 128 == 0
        fits = fits and a_count == ROWS * n_col and b_count % 8 == 0 and c_count % 8 == 0
        if fits:
            return laddered(n_dev, n_col, factor_ac, factor_bd, amplitudes)
        return plain(factor_ac, factor_bd, amplitudes)

    return jax.shard_map(
        local,
        mesh=mesh,
        in_specs=placed,
        out_specs=P(("frag", "col"), "dev", None),
        check_vma=False,
    )
```

```python
import functools

import jax
import jax.numpy as jnp
from jax import lax
from jax.experimental import pallas as pl
from jax.experimental.pallas import tpu as pltpu
from jax.sharding import PartitionSpec as P


F32 = jnp.float32
ROWS = 8
WIDE = 4
LIMIT = 24 * 2**20


def plain(factor_ac, factor_bd, amplitudes):
    whole_bd = lax.all_gather(factor_bd, "col", axis=0, tiled=True)
    whole_ac = lax.all_gather(factor_ac, "dev", axis=0, tiled=True)
    integral = jnp.einsum("qac,qbd->abdc", whole_ac, whole_bd, preferred_element_type=F32)
    integral = integral.astype(jnp.bfloat16)
    partial_sum = jnp.einsum("abdc,cdp->abp", integral, amplitudes, preferred_element_type=F32)
    reduced = lax.psum_scatter(partial_sum, "col", scatter_dimension=0, tiled=True)
    return lax.psum_scatter(reduced, "dev", scatter_dimension=1, tiled=True)


def block_kernel(first, starts, rows, c_start, where, own, near, far0, far1, end0, end1,
                 b_ref, t_ref, r_ref, out_ref, a_v, t_v, i_v, a_sem, t_sem):
    depth = own.shape[1]
    count = rows // ROWS
    b_count, _, width = b_ref.shape
    sources = (own, near, far0, far1, end0, end1)

    def a_copy(index, slot):
        source = sources[index].at[pl.ds(starts[index], rows), :]
        column = pl.ds(pl.multiple_of(where[slot] * depth, 128), depth)
        return pltpu.make_async_copy(source, a_v.at[:, column], a_sem.at[slot])

    t_copy = pltpu.make_async_copy(t_ref.at[pl.ds(c_start, count)], t_v, t_sem)
    a_copy(0, 0).start()
    a_copy(1, 1).start()

    @pl.when(where[4] == 1)
    def _():
        a_copy(4, 2).start()
        a_copy(5, 3).start()

    @pl.when(where[4] == 0)
    def _():
        a_copy(2, 2).start()
        a_copy(3, 3).start()

    t_copy.start()
    for slot in range(4):
        a_copy(slot, slot).wait()

    def contract(step, carry):
        start = step * WIDE
        right = jnp.concatenate([b_ref[start + m] for m in range(WIDE)], axis=1)
        part = jnp.dot(a_v[...], right, preferred_element_type=F32)
        part = part.reshape(count, ROWS, WIDE * width)
        tall = jnp.concatenate([part[:, :, m * width:(m + 1) * width] for m in range(WIDE)], axis=1)
        i_v[:, pl.ds(pl.multiple_of(ROWS * start, WIDE * ROWS), WIDE * ROWS), :] = tall.astype(jnp.bfloat16)
        return carry

    lax.fori_loop(0, b_count // WIDE, contract, 0)
    t_copy.wait()
    group = 8
    total = jnp.zeros(out_ref.shape, F32) if first else r_ref[...]
    for c in range(0, count, group):
        left = jnp.concatenate([i_v[c + m] for m in range(group)], axis=1)
        amp = t_v[c:c + group].reshape(group * width, t_v.shape[2])
        total += jnp.dot(left, amp, preferred_element_type=F32)
    out_ref[...] = total


def gather_kernel(b0, b1, b2, b3, out_ref, sem):
    depth = b0.shape[1]
    copies = [
        pltpu.make_async_copy(b, out_ref.at[:, pl.ds(m * depth, depth), :], sem.at[m])
        for m, b in enumerate((b0, b1, b2, b3))
    ]
    for copy in copies:
        copy.start()
    for copy in copies:
        copy.wait()


def gathered(quarters):
    b_count, depth, width = quarters[0].shape
    anywhere = pl.BlockSpec(memory_space=pl.ANY)
    return pl.pallas_call(
        gather_kernel,
        in_specs=[anywhere] * 4,
        out_specs=pl.BlockSpec(memory_space=pltpu.VMEM),
        out_shape=pltpu.VMEM((b_count, 4 * depth, width), quarters[0].dtype),
        scratch_shapes=[pltpu.SemaphoreType.DMA((4,))],
        compiler_params=pltpu.CompilerParams(vmem_limit_bytes=2**20),
    )(*quarters)


def block(first, where, pieces, starts, rows, whole_bd, amplitudes, c_start, total):
    depth = pieces[0].shape[1]
    count = rows // ROWS
    b_count, _, width = whole_bd.shape
    pairs = amplitudes.shape[2]
    q_count = depth * 4
    shape = (b_count * ROWS, pairs)
    flops = 2 * rows * q_count * b_count * width + 2 * count * width * b_count * ROWS * pairs
    anywhere = pl.BlockSpec(memory_space=pl.ANY)
    inside = pl.BlockSpec(memory_space=pltpu.VMEM)
    return pl.pallas_call(
        functools.partial(block_kernel, first, starts, rows, c_start),
        in_specs=[pl.BlockSpec(memory_space=pltpu.SMEM)] + [anywhere] * 6 + [inside, anywhere, inside],
        out_specs=inside,
        scratch_shapes=[
            pltpu.VMEM((rows, q_count), jnp.bfloat16),
            pltpu.VMEM((count, width, pairs), jnp.bfloat16),
            pltpu.VMEM((count, b_count * ROWS, width), jnp.bfloat16),
            pltpu.SemaphoreType.DMA((4,)),
            pltpu.SemaphoreType.DMA,
        ],
        out_shape=jax.ShapeDtypeStruct(shape, F32),
        compiler_params=pltpu.CompilerParams(vmem_limit_bytes=LIMIT),
        cost_estimate=pl.CostEstimate(
            flops=flops,
            transcendentals=0,
            bytes_accessed=2 * (b_count * q_count * width + count * width * pairs + rows * q_count),
        ),
    )(where, *pieces, pltpu.with_memory_space_constraint(whole_bd, pltpu.VMEM), amplitudes, total)


INNER = [(1, 2), (2, 1)]
TO_END = [(1, 0), (2, 3)]


def shuffled(n, mask):
    return [(i, i ^ mask) for i in range(n)]


def laddered(n_dev, n_col, factor_ac, factor_bd, amplitudes):
    depth, a_count, c_count = factor_ac.shape
    _, b_count, _ = factor_bd.shape
    pairs = amplitudes.shape[2]
    dev, col = lax.axis_index("dev").astype(jnp.int32), lax.axis_index("col").astype(jnp.int32)
    low = dev < 2
    outer = (dev == 0) | (dev == 3)
    order = [dev, dev ^ 1, jnp.where(low, 2, 1), jnp.where(low, 3, 0)]
    where = jnp.stack([x ^ col for x in order] + [outer.astype(jnp.int32)])
    groups = a_count // ROWS
    mid = c_count // 2
    spans = [[(0, c_count)]] * (groups - 1) + [[(0, mid), (mid, c_count)]]

    def turned(g):
        return factor_ac[:, g * ROWS:(g + 1) * ROWS].transpose(2, 1, 0).reshape(c_count * ROWS, depth)

    def ends(g, x):
        parts = [x[c0 * ROWS:c1 * ROWS] for c0, c1 in spans[g]] if len(spans[g]) > 1 else [x]
        return [lax.ppermute(part, "dev", TO_END) for part in parts]

    own = [turned(g) for g in range(groups)]
    turned_bd = factor_bd.transpose(1, 0, 2)
    near = [lax.ppermute(x, "dev", shuffled(n_dev, 1)) for x in own]
    far0 = [lax.ppermute(x, "dev", INNER) for x in own]
    far1 = [lax.ppermute(x, "dev", INNER) for x in near]
    across = lax.ppermute(turned_bd, "col", shuffled(n_col, 2))
    beside = lax.ppermute(turned_bd, "col", shuffled(n_col, 1))
    diagonal = lax.ppermute(across, "col", shuffled(n_col, 1))
    whole_bd = gathered((turned_bd, beside, across, diagonal))

    def to_owner(group, total):
        with_core = [(i, i ^ 1) for i in range(n_col) if i % 2 != group % 2]
        early = total + lax.ppermute(total, "col", with_core)
        return early + lax.ppermute(early, "col", [(group ^ 2, group)]), early

    totals = []
    for g in range(groups):
        total = jnp.zeros((b_count * ROWS, pairs), F32)
        third, fourth = far0[g], far1[g]
        if len(spans[g]) > 1:
            third, totals[0] = lax.optimization_barrier((third, totals[0]))
            fourth, totals[1] = lax.optimization_barrier((fourth, totals[1]))
        end0, end1 = ends(g, third), ends(g, fourth)
        for i, (c0, c1) in enumerate(spans[g]):
            pieces = (own[g], near[g], third, fourth, end0[i], end1[i])
            starts = (c0 * ROWS,) * 4 + (0, 0)
            total = block(i == 0, where, pieces, starts, (c1 - c0) * ROWS, whole_bd, amplitudes, c0, total)
        totals.append(total)
    mine, early = to_owner(0, totals[0])
    for group in range(1, groups):
        total, _ = lax.optimization_barrier((totals[group], early))
        whole, early = to_owner(group, total)
        mine = jnp.where(col == group, whole, mine)
    mine = mine.reshape(n_dev, b_count // n_dev * ROWS, pairs)
    out = lax.dynamic_index_in_dim(mine, dev, 0, keepdims=False)
    for mask in range(1, n_dev):
        give = lax.dynamic_index_in_dim(mine, dev ^ mask, 0, keepdims=False)
        out = out + lax.ppermute(give, "dev", shuffled(n_dev, mask))
    return out.reshape(b_count // n_dev, ROWS, pairs).transpose(1, 0, 2)


def solution(mesh):
    n_dev, n_col = mesh.shape["dev"], mesh.shape["col"]
    placed = (
        P(("frag", "dev"), None, "col"),
        P(("frag", "col"), None, "dev"),
        P(("frag", "col"), "dev", None),
    )

    def local(factor_ac, factor_bd, amplitudes):
        depth, a_count, c_count = factor_ac.shape
        _, b_count, width = factor_bd.shape
        fits = n_dev == 4 and n_col == 4 and width == 128 and depth % 128 == 0
        fits = fits and a_count == ROWS * n_col and b_count % 8 == 0 and c_count % 8 == 0
        if fits:
            return laddered(n_dev, n_col, factor_ac, factor_bd, amplitudes)
        return plain(factor_ac, factor_bd, amplitudes)

    return jax.shard_map(
        local,
        mesh=mesh,
        in_specs=placed,
        out_specs=P(("frag", "col"), "dev", None),
        check_vma=False,
    )
```

```python
import functools

import jax
import jax.numpy as jnp
from jax import lax
from jax.experimental import pallas as pl
from jax.experimental.pallas import tpu as pltpu
from jax.sharding import PartitionSpec as P


F32 = jnp.float32
ROWS = 8
WIDE = 4
LIMIT = 24 * 2**20


def plain(factor_ac, factor_bd, amplitudes):
    whole_bd = lax.all_gather(factor_bd, "col", axis=0, tiled=True)
    whole_ac = lax.all_gather(factor_ac, "dev", axis=0, tiled=True)
    integral = jnp.einsum("qac,qbd->abdc", whole_ac, whole_bd, preferred_element_type=F32)
    integral = integral.astype(jnp.bfloat16)
    partial_sum = jnp.einsum("abdc,cdp->abp", integral, amplitudes, preferred_element_type=F32)
    reduced = lax.psum_scatter(partial_sum, "col", scatter_dimension=0, tiled=True)
    return lax.psum_scatter(reduced, "dev", scatter_dimension=1, tiled=True)


def block_kernel(first, rows, c_start, where, held, far, end, b_ref, t_ref, r_ref, out_ref,
                 a_v, t_v, i_v, a_sem, t_sem):
    depth = held.shape[1]
    count = rows // ROWS
    b_count, _, width = b_ref.shape

    def a_copy(source, slot):
        span = pl.ds(slot % 2 * rows, rows)
        column = pl.ds(pl.multiple_of(where[slot] * depth, 128), depth)
        return pltpu.make_async_copy(source.at[span, :], a_v.at[:, column], a_sem.at[slot])

    t_copy = pltpu.make_async_copy(t_ref.at[pl.ds(c_start, count)], t_v, t_sem)
    a_copy(held, 0).start()
    a_copy(held, 1).start()

    @pl.when(where[4] == 1)
    def _():
        a_copy(end, 2).start()
        a_copy(end, 3).start()

    @pl.when(where[4] == 0)
    def _():
        a_copy(far, 2).start()
        a_copy(far, 3).start()

    t_copy.start()
    for slot in range(4):
        a_copy(held, slot).wait()

    def contract(step, carry):
        start = step * WIDE
        right = jnp.concatenate([b_ref[start + m] for m in range(WIDE)], axis=1)
        part = jnp.dot(a_v[...], right, preferred_element_type=F32)
        part = part.reshape(count, ROWS, WIDE * width)
        tall = jnp.concatenate([part[:, :, m * width:(m + 1) * width] for m in range(WIDE)], axis=1)
        i_v[:, pl.ds(pl.multiple_of(ROWS * start, WIDE * ROWS), WIDE * ROWS), :] = tall.astype(jnp.bfloat16)
        return carry

    lax.fori_loop(0, b_count // WIDE, contract, 0)
    t_copy.wait()
    group = 8
    total = jnp.zeros(out_ref.shape, F32) if first else r_ref[...]
    for c in range(0, count, group):
        left = jnp.concatenate([i_v[c + m] for m in range(group)], axis=1)
        amp = t_v[c:c + group].reshape(group * width, t_v.shape[2])
        total += jnp.dot(left, amp, preferred_element_type=F32)
    out_ref[...] = total


def gather_kernel(b0, b1, b2, b3, out_ref, token_ref, sem):
    depth = b0.shape[1]
    token_ref[...] = jnp.zeros(token_ref.shape, F32)
    copies = [
        pltpu.make_async_copy(b, out_ref.at[:, pl.ds(m * depth, depth), :], sem.at[m])
        for m, b in enumerate((b0, b1, b2, b3))
    ]
    for copy in copies:
        copy.start()
    for copy in copies:
        copy.wait()


def gathered(quarters):
    b_count, depth, width = quarters[0].shape
    anywhere = pl.BlockSpec(memory_space=pl.ANY)
    return pl.pallas_call(
        gather_kernel,
        in_specs=[anywhere] * 4,
        out_specs=[pl.BlockSpec(memory_space=pltpu.VMEM)] * 2,
        out_shape=[
            pltpu.VMEM((b_count, 4 * depth, width), quarters[0].dtype),
            jax.ShapeDtypeStruct((8, 128), F32),
        ],
        scratch_shapes=[pltpu.SemaphoreType.DMA((4,))],
        compiler_params=pltpu.CompilerParams(vmem_limit_bytes=2**20),
    )(*quarters)


def block(first, where, pieces, whole_bd, amplitudes, c_start, total):
    rows, depth = pieces[0].shape[0] // 2, pieces[0].shape[1]
    count = rows // ROWS
    b_count, _, width = whole_bd.shape
    pairs = amplitudes.shape[2]
    q_count = depth * 4
    shape = (b_count * ROWS, pairs)
    flops = 2 * rows * q_count * b_count * width + 2 * count * width * b_count * ROWS * pairs
    anywhere = pl.BlockSpec(memory_space=pl.ANY)
    inside = pl.BlockSpec(memory_space=pltpu.VMEM)
    return pl.pallas_call(
        functools.partial(block_kernel, first, rows, c_start),
        in_specs=[pl.BlockSpec(memory_space=pltpu.SMEM)] + [anywhere] * 3 + [inside, anywhere, inside],
        out_specs=inside,
        scratch_shapes=[
            pltpu.VMEM((rows, q_count), jnp.bfloat16),
            pltpu.VMEM((count, width, pairs), jnp.bfloat16),
            pltpu.VMEM((count, b_count * ROWS, width), jnp.bfloat16),
            pltpu.SemaphoreType.DMA((4,)),
            pltpu.SemaphoreType.DMA,
        ],
        out_shape=jax.ShapeDtypeStruct(shape, F32),
        compiler_params=pltpu.CompilerParams(vmem_limit_bytes=LIMIT),
        cost_estimate=pl.CostEstimate(
            flops=flops,
            transcendentals=0,
            bytes_accessed=2 * (b_count * q_count * width + count * width * pairs + rows * q_count),
        ),
    )(where, *pieces, pltpu.with_memory_space_constraint(whole_bd, pltpu.VMEM), amplitudes, total)


INNER = [(1, 2), (2, 1)]
TO_END = [(1, 0), (2, 3)]


def shuffled(n, mask):
    return [(i, i ^ mask) for i in range(n)]


def laddered(n_dev, n_col, factor_ac, factor_bd, amplitudes):
    depth, a_count, c_count = factor_ac.shape
    _, b_count, _ = factor_bd.shape
    pairs = amplitudes.shape[2]
    dev, col = lax.axis_index("dev").astype(jnp.int32), lax.axis_index("col").astype(jnp.int32)
    low = dev < 2
    outer = (dev == 0) | (dev == 3)
    order = [dev, dev ^ 1, jnp.where(low, 2, 1), jnp.where(low, 3, 0)]
    where = jnp.stack([x ^ col for x in order] + [outer.astype(jnp.int32)])
    groups = a_count // ROWS
    eighth = c_count // 8
    cuts = [(0, 8), (0, 8), (0, 4, 8), (0, 3, 6, 8)]
    spans = [[(p * eighth, q * eighth) for p, q in zip(cut, cut[1:])] for cut in cuts]

    def raw(g):
        return factor_ac[:, g * ROWS:(g + 1) * ROWS]

    def turned(x):
        return lax.optimization_barrier(x.transpose(2, 1, 0).reshape(c_count * ROWS, depth))

    first = lax.optimization_barrier(raw(0))
    own = [turned(first)] + [turned(raw(g)) for g in range(1, groups)]
    turned_bd = factor_bd.transpose(1, 0, 2)
    near = [turned(lax.ppermute(first, "dev", shuffled(n_dev, 1)))]
    near += [lax.ppermute(own[g], "dev", shuffled(n_dev, 1)) for g in range(1, groups)]
    across = lax.ppermute(turned_bd, "col", shuffled(n_col, 2))
    beside = lax.ppermute(turned_bd, "col", shuffled(n_col, 1))
    diagonal = lax.ppermute(across, "col", shuffled(n_col, 1))
    whole_bd, token = gathered((turned_bd, beside, across, diagonal))

    core, chip = col % 2, col // 2

    def paired(even, odd):
        keep, give = jnp.where(core == 0, even, odd), jnp.where(core == 0, odd, even)
        return keep + lax.ppermute(give, "col", shuffled(n_col, 1))

    totals = [jnp.zeros((b_count * ROWS, pairs), F32)] * groups
    ready = []

    def send(g, *gates):
        mine, other, *_ = lax.optimization_barrier((own[g], near[g], *gates))
        for i, (c0, c1) in enumerate(spans[g]):
            held = jnp.concatenate([x[c0 * ROWS:c1 * ROWS] for x in (mine, other)], axis=0)
            far = lax.ppermute(held, "dev", INNER)
            ready.append((g, i, c0, held, far, lax.ppermute(far, "dev", TO_END)))

    def work(g):
        for h, i, c0, *parts in ready:
            if h == g:
                totals[g] = block(i == 0, where, parts, whole_bd, amplitudes, c0, totals[g])
        return totals[g]

    send(0)
    send(1)
    send(2, token)
    send(3, work(0))
    for g in range(1, groups):
        work(g)
    lower = paired(totals[0], totals[1])
    even, odd, _ = lax.optimization_barrier((totals[2], totals[3], lower))
    upper = paired(even, odd)
    keep, give = jnp.where(chip == 0, lower, upper), jnp.where(chip == 0, upper, lower)
    mine = keep + lax.ppermute(give, "col", shuffled(n_col, 2))
    mine = mine.reshape(n_dev, b_count // n_dev * ROWS, pairs)
    out = lax.dynamic_index_in_dim(mine, dev, 0, keepdims=False)
    for mask in range(1, n_dev):
        give = lax.dynamic_index_in_dim(mine, dev ^ mask, 0, keepdims=False)
        out = out + lax.ppermute(give, "dev", shuffled(n_dev, mask))
    return out.reshape(b_count // n_dev, ROWS, pairs).transpose(1, 0, 2)


def solution(mesh):
    n_dev, n_col = mesh.shape["dev"], mesh.shape["col"]
    placed = (
        P(("frag", "dev"), None, "col"),
        P(("frag", "col"), None, "dev"),
        P(("frag", "col"), "dev", None),
    )

    def local(factor_ac, factor_bd, amplitudes):
        depth, a_count, c_count = factor_ac.shape
        _, b_count, width = factor_bd.shape
        fits = n_dev == 4 and n_col == 4 and width == 128 and depth % 128 == 0
        fits = fits and a_count == ROWS * n_col and b_count % 8 == 0 and c_count % 64 == 0
        if fits:
            return laddered(n_dev, n_col, factor_ac, factor_bd, amplitudes)
        return plain(factor_ac, factor_bd, amplitudes)

    return jax.shard_map(
        local,
        mesh=mesh,
        in_specs=placed,
        out_specs=P(("frag", "col"), "dev", None),
        check_vma=False,
    )
```

```python
import functools

import jax
import jax.numpy as jnp
from jax import lax
from jax.experimental import pallas as pl
from jax.experimental.pallas import tpu as pltpu
from jax.sharding import PartitionSpec as P


F32 = jnp.float32
ROWS = 8
WIDE = 8
LIMIT = 24 * 2**20


def plain(factor_ac, factor_bd, amplitudes):
    whole_bd = lax.all_gather(factor_bd, "col", axis=0, tiled=True)
    whole_ac = lax.all_gather(factor_ac, "dev", axis=0, tiled=True)
    integral = jnp.einsum("qac,qbd->abdc", whole_ac, whole_bd, preferred_element_type=F32)
    integral = integral.astype(jnp.bfloat16)
    partial_sum = jnp.einsum("abdc,cdp->abp", integral, amplitudes, preferred_element_type=F32)
    reduced = lax.psum_scatter(partial_sum, "col", scatter_dimension=0, tiled=True)
    return lax.psum_scatter(reduced, "dev", scatter_dimension=1, tiled=True)


def block_kernel(first, rows, c_start, where, held, far, end, b_ref, t_ref, r_ref, out_ref,
                 a_v, t_v, i_v, a_sem, t_sem):
    depth = held.shape[1]
    count = rows // ROWS
    b_count, _, width = b_ref.shape

    def a_copy(source, slot):
        span = pl.ds(slot % 2 * rows, rows)
        column = pl.ds(pl.multiple_of(where[slot] * depth, 128), depth)
        return pltpu.make_async_copy(source.at[span, :], a_v.at[:, column], a_sem.at[slot])

    t_copy = pltpu.make_async_copy(t_ref.at[pl.ds(c_start, count)], t_v, t_sem)
    a_copy(held, 0).start()
    a_copy(held, 1).start()

    @pl.when(where[4] == 1)
    def _():
        a_copy(end, 2).start()
        a_copy(end, 3).start()

    @pl.when(where[4] == 0)
    def _():
        a_copy(far, 2).start()
        a_copy(far, 3).start()

    t_copy.start()
    for slot in range(4):
        a_copy(held, slot).wait()

    def contract(step, carry):
        start = step * WIDE
        right = jnp.concatenate([b_ref[start + m] for m in range(WIDE)], axis=1)
        part = jnp.dot(a_v[...], right, preferred_element_type=F32)
        part = part.reshape(count, ROWS, WIDE * width)
        tall = jnp.concatenate([part[:, :, m * width:(m + 1) * width] for m in range(WIDE)], axis=1)
        i_v[:, pl.ds(pl.multiple_of(ROWS * start, WIDE * ROWS), WIDE * ROWS), :] = tall.astype(jnp.bfloat16)
        return carry

    lax.fori_loop(0, b_count // WIDE, contract, 0)
    t_copy.wait()
    group = 8
    total = jnp.zeros(out_ref.shape, F32) if first else r_ref[...]
    for c in range(0, count, group):
        left = jnp.concatenate([i_v[c + m] for m in range(group)], axis=1)
        amp = t_v[c:c + group].reshape(group * width, t_v.shape[2])
        total += jnp.dot(left, amp, preferred_element_type=F32)
    out_ref[...] = total


def gather_kernel(b0, b1, b2, b3, out_ref, token_ref, sem):
    depth = b0.shape[1]
    token_ref[...] = jnp.zeros(token_ref.shape, F32)
    copies = [
        pltpu.make_async_copy(b, out_ref.at[:, pl.ds(m * depth, depth), :], sem.at[m])
        for m, b in enumerate((b0, b1, b2, b3))
    ]
    for copy in copies:
        copy.start()
    for copy in copies:
        copy.wait()


def gathered(quarters):
    b_count, depth, width = quarters[0].shape
    anywhere = pl.BlockSpec(memory_space=pl.ANY)
    return pl.pallas_call(
        gather_kernel,
        in_specs=[anywhere] * 4,
        out_specs=[pl.BlockSpec(memory_space=pltpu.VMEM)] * 2,
        out_shape=[
            pltpu.VMEM((b_count, 4 * depth, width), quarters[0].dtype),
            jax.ShapeDtypeStruct((8, 128), F32),
        ],
        scratch_shapes=[pltpu.SemaphoreType.DMA((4,))],
        compiler_params=pltpu.CompilerParams(vmem_limit_bytes=2**20),
    )(*quarters)


def block(first, where, pieces, whole_bd, amplitudes, c_start, total):
    rows, depth = pieces[0].shape[0] // 2, pieces[0].shape[1]
    count = rows // ROWS
    b_count, _, width = whole_bd.shape
    pairs = amplitudes.shape[2]
    q_count = depth * 4
    shape = (b_count * ROWS, pairs)
    flops = 2 * rows * q_count * b_count * width + 2 * count * width * b_count * ROWS * pairs
    anywhere = pl.BlockSpec(memory_space=pl.ANY)
    inside = pl.BlockSpec(memory_space=pltpu.VMEM)
    return pl.pallas_call(
        functools.partial(block_kernel, first, rows, c_start),
        in_specs=[pl.BlockSpec(memory_space=pltpu.SMEM)] + [anywhere] * 3 + [inside, anywhere, inside],
        out_specs=inside,
        scratch_shapes=[
            pltpu.VMEM((rows, q_count), jnp.bfloat16),
            pltpu.VMEM((count, width, pairs), jnp.bfloat16),
            pltpu.VMEM((count, b_count * ROWS, width), jnp.bfloat16),
            pltpu.SemaphoreType.DMA((4,)),
            pltpu.SemaphoreType.DMA,
        ],
        out_shape=jax.ShapeDtypeStruct(shape, F32),
        compiler_params=pltpu.CompilerParams(vmem_limit_bytes=LIMIT),
        cost_estimate=pl.CostEstimate(
            flops=flops,
            transcendentals=0,
            bytes_accessed=2 * (b_count * q_count * width + count * width * pairs + rows * q_count),
        ),
    )(where, *pieces, pltpu.with_memory_space_constraint(whole_bd, pltpu.VMEM), amplitudes, total)


INNER = [(1, 2), (2, 1)]
TO_END = [(1, 0), (2, 3)]


def shuffled(n, mask):
    return [(i, i ^ mask) for i in range(n)]


def laddered(n_dev, n_col, factor_ac, factor_bd, amplitudes):
    depth, a_count, c_count = factor_ac.shape
    _, b_count, _ = factor_bd.shape
    pairs = amplitudes.shape[2]
    dev, col = lax.axis_index("dev").astype(jnp.int32), lax.axis_index("col").astype(jnp.int32)
    low = dev < 2
    outer = (dev == 0) | (dev == 3)
    order = [dev, dev ^ 1, jnp.where(low, 2, 1), jnp.where(low, 3, 0)]
    where = jnp.stack([x ^ col for x in order] + [outer.astype(jnp.int32)])
    groups = a_count // ROWS
    eighth = c_count // 8
    cuts = [(0, 8), (0, 8), (0, 4, 8), (0, 3, 6, 8)]
    spans = [[(p * eighth, q * eighth) for p, q in zip(cut, cut[1:])] for cut in cuts]

    turns = (0, 2, 1, 3)

    def raw(g):
        return factor_ac[:, turns[g] * ROWS:(turns[g] + 1) * ROWS]

    def turned(x):
        return lax.optimization_barrier(x.transpose(2, 1, 0).reshape(c_count * ROWS, depth))

    first = lax.optimization_barrier(raw(0))
    own = [turned(first)] + [turned(raw(g)) for g in range(1, groups)]
    turned_bd = factor_bd.transpose(1, 0, 2)
    near = [turned(lax.ppermute(first, "dev", shuffled(n_dev, 1)))]
    near += [lax.ppermute(own[g], "dev", shuffled(n_dev, 1)) for g in range(1, groups)]
    across = lax.ppermute(turned_bd, "col", shuffled(n_col, 2))
    beside = lax.ppermute(turned_bd, "col", shuffled(n_col, 1))
    diagonal = lax.ppermute(across, "col", shuffled(n_col, 1))
    whole_bd, token = gathered((turned_bd, beside, across, diagonal))

    core, chip = col % 2, col // 2

    def joined(keeper, pair):
        away = [(i, i ^ 1) for i in range(n_col) if i % 2 != keeper]
        across_chips = [(i, i ^ 2) for i in range(n_col) if i % 2 == keeper]
        both = jnp.stack(pair)
        both = both + lax.ppermute(both, "col", away)
        give = lax.dynamic_index_in_dim(both, 1 - chip, 0, keepdims=False)
        keep = lax.dynamic_index_in_dim(both, chip, 0, keepdims=False)
        return keep + lax.ppermute(give, "col", across_chips)

    totals = [jnp.zeros((b_count * ROWS, pairs), F32)] * groups
    ready = []

    def send(g, *gates):
        mine, other, *_ = lax.optimization_barrier((own[g], near[g], *gates))
        for i, (c0, c1) in enumerate(spans[g]):
            held = jnp.concatenate([x[c0 * ROWS:c1 * ROWS] for x in (mine, other)], axis=0)
            far = lax.ppermute(held, "dev", INNER)
            ready.append((g, i, c0, held, far, lax.ppermute(far, "dev", TO_END)))

    def work(g):
        for h, i, c0, *parts in ready:
            if h == g:
                totals[g] = block(i == 0, where, parts, whole_bd, amplitudes, c0, totals[g])
        return totals[g]

    send(0)
    send(1)
    send(2, token)
    send(3, work(0))
    for g in range(1, groups):
        work(g)
    lower = joined(0, totals[:2])
    third, fourth, lower = lax.optimization_barrier((totals[2], totals[3], lower))
    mine = jnp.where(core == 0, lower, joined(1, [third, fourth]))
    mine = mine.reshape(n_dev, b_count // n_dev * ROWS, pairs)
    out = lax.dynamic_index_in_dim(mine, dev, 0, keepdims=False)
    for mask in (3, 2, 1):
        give = lax.dynamic_index_in_dim(mine, dev ^ mask, 0, keepdims=False)
        out = out + lax.ppermute(give, "dev", shuffled(n_dev, mask))
    return out.reshape(b_count // n_dev, ROWS, pairs).transpose(1, 0, 2)


def solution(mesh):
    n_dev, n_col = mesh.shape["dev"], mesh.shape["col"]
    placed = (
        P(("frag", "dev"), None, "col"),
        P(("frag", "col"), None, "dev"),
        P(("frag", "col"), "dev", None),
    )

    def local(factor_ac, factor_bd, amplitudes):
        depth, a_count, c_count = factor_ac.shape
        _, b_count, width = factor_bd.shape
        fits = n_dev == 4 and n_col == 4 and width == 128 and depth % 128 == 0
        fits = fits and a_count == ROWS * n_col and b_count % 8 == 0 and c_count % 64 == 0
        if fits:
            return laddered(n_dev, n_col, factor_ac, factor_bd, amplitudes)
        return plain(factor_ac, factor_bd, amplitudes)

    return jax.shard_map(
        local,
        mesh=mesh,
        in_specs=placed,
        out_specs=P(("frag", "col"), "dev", None),
        check_vma=False,
    )
```

```python
import functools

import jax
import jax.numpy as jnp
from jax import lax
from jax.experimental import pallas as pl
from jax.experimental.pallas import tpu as pltpu
from jax.sharding import PartitionSpec as P


F32 = jnp.float32
ROWS = 8
WIDE = 8
LIMIT = 24 * 2**20


def plain(factor_ac, factor_bd, amplitudes):
    whole_bd = lax.all_gather(factor_bd, "col", axis=0, tiled=True)
    whole_ac = lax.all_gather(factor_ac, "dev", axis=0, tiled=True)
    integral = jnp.einsum("qac,qbd->abdc", whole_ac, whole_bd, preferred_element_type=F32)
    integral = integral.astype(jnp.bfloat16)
    partial_sum = jnp.einsum("abdc,cdp->abp", integral, amplitudes, preferred_element_type=F32)
    reduced = lax.psum_scatter(partial_sum, "col", scatter_dimension=0, tiled=True)
    return lax.psum_scatter(reduced, "dev", scatter_dimension=1, tiled=True)


def block_kernel(first, rows, c_start, where, held, far, end, b_ref, t_ref, r_ref, out_ref,
                 a_v, t_v, i_v, a_sem, t_sem):
    depth = held.shape[1]
    count = rows // ROWS
    b_count, _, width = b_ref.shape

    def a_copy(source, slot):
        span = pl.ds(slot % 2 * rows, rows)
        column = pl.ds(pl.multiple_of(where[slot] * depth, 128), depth)
        return pltpu.make_async_copy(source.at[span, :], a_v.at[:, column], a_sem.at[slot])

    t_copy = pltpu.make_async_copy(t_ref.at[pl.ds(c_start, count)], t_v, t_sem)
    a_copy(held, 0).start()
    a_copy(held, 1).start()

    @pl.when(where[4] == 1)
    def _():
        a_copy(end, 2).start()
        a_copy(end, 3).start()

    @pl.when(where[4] == 0)
    def _():
        a_copy(far, 2).start()
        a_copy(far, 3).start()

    t_copy.start()
    for slot in range(4):
        a_copy(held, slot).wait()

    def contract(step, carry):
        start = step * WIDE
        right = jnp.concatenate([b_ref[start + m] for m in range(WIDE)], axis=1)
        part = jnp.dot(a_v[...], right, preferred_element_type=F32)
        part = part.reshape(count, ROWS, WIDE * width)
        tall = jnp.concatenate([part[:, :, m * width:(m + 1) * width] for m in range(WIDE)], axis=1)
        i_v[:, pl.ds(pl.multiple_of(ROWS * start, WIDE * ROWS), WIDE * ROWS), :] = tall.astype(jnp.bfloat16)
        return carry

    lax.fori_loop(0, b_count // WIDE, contract, 0)
    t_copy.wait()
    group = 8
    total = jnp.zeros(out_ref.shape, F32) if first else r_ref[...]
    for c in range(0, count, group):
        left = jnp.concatenate([i_v[c + m] for m in range(group)], axis=1)
        amp = t_v[c:c + group].reshape(group * width, t_v.shape[2])
        total += jnp.dot(left, amp, preferred_element_type=F32)
    out_ref[...] = total


def gather_kernel(b0, b1, b2, b3, out_ref, token_ref, sem):
    depth = b0.shape[1]
    token_ref[...] = jnp.zeros(token_ref.shape, F32)
    copies = [
        pltpu.make_async_copy(b, out_ref.at[:, pl.ds(m * depth, depth), :], sem.at[m])
        for m, b in enumerate((b0, b1, b2, b3))
    ]
    for copy in copies:
        copy.start()
    for copy in copies:
        copy.wait()


def gathered(quarters):
    b_count, depth, width = quarters[0].shape
    anywhere = pl.BlockSpec(memory_space=pl.ANY)
    return pl.pallas_call(
        gather_kernel,
        in_specs=[anywhere] * 4,
        out_specs=[pl.BlockSpec(memory_space=pltpu.VMEM)] * 2,
        out_shape=[
            pltpu.VMEM((b_count, 4 * depth, width), quarters[0].dtype),
            jax.ShapeDtypeStruct((8, 128), F32),
        ],
        scratch_shapes=[pltpu.SemaphoreType.DMA((4,))],
        compiler_params=pltpu.CompilerParams(vmem_limit_bytes=2**20),
    )(*quarters)


def block(first, where, pieces, whole_bd, amplitudes, c_start, total):
    rows, depth = pieces[0].shape[0] // 2, pieces[0].shape[1]
    count = rows // ROWS
    b_count, _, width = whole_bd.shape
    pairs = amplitudes.shape[2]
    q_count = depth * 4
    shape = (b_count * ROWS, pairs)
    flops = 2 * rows * q_count * b_count * width + 2 * count * width * b_count * ROWS * pairs
    anywhere = pl.BlockSpec(memory_space=pl.ANY)
    inside = pl.BlockSpec(memory_space=pltpu.VMEM)
    return pl.pallas_call(
        functools.partial(block_kernel, first, rows, c_start),
        in_specs=[pl.BlockSpec(memory_space=pltpu.SMEM)] + [anywhere] * 3 + [inside, anywhere, inside],
        out_specs=inside,
        scratch_shapes=[
            pltpu.VMEM((rows, q_count), jnp.bfloat16),
            pltpu.VMEM((count, width, pairs), jnp.bfloat16),
            pltpu.VMEM((count, b_count * ROWS, width), jnp.bfloat16),
            pltpu.SemaphoreType.DMA((4,)),
            pltpu.SemaphoreType.DMA,
        ],
        out_shape=jax.ShapeDtypeStruct(shape, F32),
        compiler_params=pltpu.CompilerParams(vmem_limit_bytes=LIMIT),
        cost_estimate=pl.CostEstimate(
            flops=flops,
            transcendentals=0,
            bytes_accessed=2 * (b_count * q_count * width + count * width * pairs + rows * q_count),
        ),
    )(where, *pieces, pltpu.with_memory_space_constraint(whole_bd, pltpu.VMEM), amplitudes, total)


INNER = [(1, 2), (2, 1)]
TO_END = [(1, 0), (2, 3)]


def shuffled(n, mask):
    return [(i, i ^ mask) for i in range(n)]


def laddered(n_dev, n_col, factor_ac, factor_bd, amplitudes):
    depth, a_count, c_count = factor_ac.shape
    _, b_count, _ = factor_bd.shape
    pairs = amplitudes.shape[2]
    dev, col = lax.axis_index("dev").astype(jnp.int32), lax.axis_index("col").astype(jnp.int32)
    low = dev < 2
    outer = (dev == 0) | (dev == 3)
    order = [dev, dev ^ 1, jnp.where(low, 2, 1), jnp.where(low, 3, 0)]
    where = jnp.stack([x ^ col for x in order] + [outer.astype(jnp.int32)])
    groups = a_count // ROWS
    eighth = c_count // 8
    cuts = [(0, 8), (0, 8), (0, 4, 8), (0, 3, 6, 8)]
    spans = [[(p * eighth, q * eighth) for p, q in zip(cut, cut[1:])] for cut in cuts]

    turns = (0, 2, 1, 3)

    def raw(g):
        return factor_ac[:, turns[g] * ROWS:(turns[g] + 1) * ROWS]

    def turned(x):
        return lax.optimization_barrier(x.transpose(2, 1, 0).reshape(c_count * ROWS, depth))

    first = lax.optimization_barrier(raw(0))
    own = [turned(first)] + [turned(raw(g)) for g in range(1, groups)]
    turned_bd = factor_bd.transpose(1, 0, 2)
    near = [turned(lax.ppermute(first, "dev", shuffled(n_dev, 1)))]
    near += [lax.ppermute(own[g], "dev", shuffled(n_dev, 1)) for g in range(1, groups)]
    across = lax.ppermute(turned_bd, "col", shuffled(n_col, 2))
    beside = lax.ppermute(turned_bd, "col", shuffled(n_col, 1))
    diagonal = lax.ppermute(across, "col", shuffled(n_col, 1))
    whole_bd, token = gathered((turned_bd, beside, across, diagonal))

    core, chip = col % 2, col // 2

    def joined(keeper, pair):
        away = [(i, i ^ 1) for i in range(n_col) if i % 2 != keeper]
        across_chips = [(i, i ^ 2) for i in range(n_col) if i % 2 == keeper]
        both = jnp.stack(pair)
        both = both + lax.ppermute(both, "col", away)
        give = lax.dynamic_index_in_dim(both, 1 - chip, 0, keepdims=False)
        keep = lax.dynamic_index_in_dim(both, chip, 0, keepdims=False)
        return keep + lax.ppermute(give, "col", across_chips)

    totals = [jnp.zeros((b_count * ROWS, pairs), F32)] * groups
    ready = []

    def send(g, *gates):
        mine, other, *_ = lax.optimization_barrier((own[g], near[g], *gates))
        for i, (c0, c1) in enumerate(spans[g]):
            held = jnp.concatenate([x[c0 * ROWS:c1 * ROWS] for x in (mine, other)], axis=0)
            far = lax.ppermute(held, "dev", INNER)
            ready.append((g, i, c0, held, far, lax.ppermute(far, "dev", TO_END)))

    def work(g):
        for h, i, c0, *parts in ready:
            if h == g:
                totals[g] = block(i == 0, where, parts, whole_bd, amplitudes, c0, totals[g])
        return totals[g]

    send(0)
    send(1)
    send(2, token)
    send(3, work(0))
    for g in range(1, groups):
        work(g)
    lower = joined(0, totals[:2])
    third, lower = lax.optimization_barrier((totals[2], lower))
    away = [(i, i ^ 1) for i in range(n_col) if i % 2 == 0]
    third = third + lax.ppermute(third, "col", away)
    fourth, third = lax.optimization_barrier((totals[3], third))
    fourth = fourth + lax.ppermute(fourth, "col", away)
    keep, give = jnp.where(chip == 0, third, fourth), jnp.where(chip == 0, fourth, third)
    upper = keep + lax.ppermute(give, "col", [(i, i ^ 2) for i in range(n_col) if i % 2 == 1])
    mine = jnp.where(core == 0, lower, upper)
    mine = mine.reshape(n_dev, b_count // n_dev * ROWS, pairs)
    out = lax.dynamic_index_in_dim(mine, dev, 0, keepdims=False)
    for mask in (3, 2, 1):
        give = lax.dynamic_index_in_dim(mine, dev ^ mask, 0, keepdims=False)
        out = out + lax.ppermute(give, "dev", shuffled(n_dev, mask))
    return out.reshape(b_count // n_dev, ROWS, pairs).transpose(1, 0, 2)


def solution(mesh):
    n_dev, n_col = mesh.shape["dev"], mesh.shape["col"]
    placed = (
        P(("frag", "dev"), None, "col"),
        P(("frag", "col"), None, "dev"),
        P(("frag", "col"), "dev", None),
    )

    def local(factor_ac, factor_bd, amplitudes):
        depth, a_count, c_count = factor_ac.shape
        _, b_count, width = factor_bd.shape
        fits = n_dev == 4 and n_col == 4 and width == 128 and depth % 128 == 0
        fits = fits and a_count == ROWS * n_col and b_count % 8 == 0 and c_count % 64 == 0
        if fits:
            return laddered(n_dev, n_col, factor_ac, factor_bd, amplitudes)
        return plain(factor_ac, factor_bd, amplitudes)

    return jax.shard_map(
        local,
        mesh=mesh,
        in_specs=placed,
        out_specs=P(("frag", "col"), "dev", None),
        check_vma=False,
    )
```

```python
import functools

import jax
import jax.numpy as jnp
from jax import lax
from jax.experimental import pallas as pl
from jax.experimental.pallas import tpu as pltpu
from jax.sharding import PartitionSpec as P


F32 = jnp.float32
ROWS = 8
WIDE = 16
LIMIT = 24 * 2**20


def plain(factor_ac, factor_bd, amplitudes):
    whole_bd = lax.all_gather(factor_bd, "col", axis=0, tiled=True)
    whole_ac = lax.all_gather(factor_ac, "dev", axis=0, tiled=True)
    integral = jnp.einsum("qac,qbd->abdc", whole_ac, whole_bd, preferred_element_type=F32)
    integral = integral.astype(jnp.bfloat16)
    partial_sum = jnp.einsum("abdc,cdp->abp", integral, amplitudes, preferred_element_type=F32)
    reduced = lax.psum_scatter(partial_sum, "col", scatter_dimension=0, tiled=True)
    return lax.psum_scatter(reduced, "dev", scatter_dimension=1, tiled=True)


def block_kernel(first, rows, c_start, where, held, far, end, b_ref, t_ref, r_ref, out_ref,
                 a_v, t_v, i_v, a_sem, t_sem):
    depth = held.shape[1]
    count = rows // ROWS
    b_count, _, width = b_ref.shape

    def a_copy(source, slot):
        span = pl.ds(slot % 2 * rows, rows)
        column = pl.ds(pl.multiple_of(where[slot] * depth, 128), depth)
        return pltpu.make_async_copy(source.at[span, :], a_v.at[:, column], a_sem.at[slot])

    t_copy = pltpu.make_async_copy(t_ref.at[pl.ds(c_start, count)], t_v, t_sem)
    a_copy(held, 0).start()
    a_copy(held, 1).start()

    @pl.when(where[4] == 1)
    def _():
        a_copy(end, 2).start()
        a_copy(end, 3).start()

    @pl.when(where[4] == 0)
    def _():
        a_copy(far, 2).start()
        a_copy(far, 3).start()

    t_copy.start()
    for slot in range(4):
        a_copy(held, slot).wait()

    def contract(step, carry):
        start = step * WIDE
        right = jnp.concatenate([b_ref[start + m] for m in range(WIDE)], axis=1)
        part = jnp.dot(a_v[...], right, preferred_element_type=F32)
        part = part.reshape(count, ROWS, WIDE * width)
        tall = jnp.concatenate([part[:, :, m * width:(m + 1) * width] for m in range(WIDE)], axis=1)
        i_v[:, pl.ds(pl.multiple_of(ROWS * start, WIDE * ROWS), WIDE * ROWS), :] = tall.astype(jnp.bfloat16)
        return carry

    lax.fori_loop(0, b_count // WIDE, contract, 0)
    t_copy.wait()
    group = 16
    total = jnp.zeros(out_ref.shape, F32) if first else r_ref[...]
    for c in range(0, count, group):
        left = jnp.concatenate([i_v[c + m] for m in range(group)], axis=1)
        amp = t_v[c:c + group].reshape(group * width, t_v.shape[2])
        total += jnp.dot(left, amp, preferred_element_type=F32)
    out_ref[...] = total


def gather_kernel(b0, b1, b2, b3, out_ref, token_ref, sem):
    depth = b0.shape[1]
    token_ref[...] = jnp.zeros(token_ref.shape, F32)
    copies = [
        pltpu.make_async_copy(b, out_ref.at[:, pl.ds(m * depth, depth), :], sem.at[m])
        for m, b in enumerate((b0, b1, b2, b3))
    ]
    for copy in copies:
        copy.start()
    for copy in copies:
        copy.wait()


def gathered(quarters):
    b_count, depth, width = quarters[0].shape
    anywhere = pl.BlockSpec(memory_space=pl.ANY)
    return pl.pallas_call(
        gather_kernel,
        in_specs=[anywhere] * 4,
        out_specs=[pl.BlockSpec(memory_space=pltpu.VMEM)] * 2,
        out_shape=[
            pltpu.VMEM((b_count, 4 * depth, width), quarters[0].dtype),
            jax.ShapeDtypeStruct((8, 128), F32),
        ],
        scratch_shapes=[pltpu.SemaphoreType.DMA((4,))],
        compiler_params=pltpu.CompilerParams(vmem_limit_bytes=2**20),
    )(*quarters)


def block(first, where, pieces, whole_bd, amplitudes, c_start, total):
    rows, depth = pieces[0].shape[0] // 2, pieces[0].shape[1]
    count = rows // ROWS
    b_count, _, width = whole_bd.shape
    pairs = amplitudes.shape[2]
    q_count = depth * 4
    shape = (b_count * ROWS, pairs)
    flops = 2 * rows * q_count * b_count * width + 2 * count * width * b_count * ROWS * pairs
    anywhere = pl.BlockSpec(memory_space=pl.ANY)
    inside = pl.BlockSpec(memory_space=pltpu.VMEM)
    return pl.pallas_call(
        functools.partial(block_kernel, first, rows, c_start),
        in_specs=[pl.BlockSpec(memory_space=pltpu.SMEM)] + [anywhere] * 3 + [inside, anywhere, inside],
        out_specs=inside,
        scratch_shapes=[
            pltpu.VMEM((rows, q_count), jnp.bfloat16),
            pltpu.VMEM((count, width, pairs), jnp.bfloat16),
            pltpu.VMEM((count, b_count * ROWS, width), jnp.bfloat16),
            pltpu.SemaphoreType.DMA((4,)),
            pltpu.SemaphoreType.DMA,
        ],
        out_shape=jax.ShapeDtypeStruct(shape, F32),
        compiler_params=pltpu.CompilerParams(vmem_limit_bytes=LIMIT),
        cost_estimate=pl.CostEstimate(
            flops=flops,
            transcendentals=0,
            bytes_accessed=2 * (b_count * q_count * width + count * width * pairs + rows * q_count),
        ),
    )(where, *pieces, pltpu.with_memory_space_constraint(whole_bd, pltpu.VMEM), amplitudes, total)


INNER = [(1, 2), (2, 1)]
TO_END = [(1, 0), (2, 3)]


def shuffled(n, mask):
    return [(i, i ^ mask) for i in range(n)]


def laddered(n_dev, n_col, factor_ac, factor_bd, amplitudes):
    depth, a_count, c_count = factor_ac.shape
    _, b_count, _ = factor_bd.shape
    pairs = amplitudes.shape[2]
    dev, col = lax.axis_index("dev").astype(jnp.int32), lax.axis_index("col").astype(jnp.int32)
    low = dev < 2
    outer = (dev == 0) | (dev == 3)
    order = [dev, dev ^ 1, jnp.where(low, 2, 1), jnp.where(low, 3, 0)]
    where = jnp.stack([x ^ col for x in order] + [outer.astype(jnp.int32)])
    groups = a_count // ROWS
    eighth = c_count // 8
    cuts = [(0, 8), (0, 8), (0, 4, 8), (0, 3, 6, 8)]
    spans = [[(p * eighth, q * eighth) for p, q in zip(cut, cut[1:])] for cut in cuts]

    turns = (0, 2, 1, 3)

    def raw(g):
        return factor_ac[:, turns[g] * ROWS:(turns[g] + 1) * ROWS]

    def turned(x):
        return lax.optimization_barrier(x.transpose(2, 1, 0).reshape(c_count * ROWS, depth))

    first = lax.optimization_barrier(raw(0))
    own = [turned(first)] + [turned(raw(g)) for g in range(1, groups)]
    turned_bd = factor_bd.transpose(1, 0, 2)
    near = [turned(lax.ppermute(first, "dev", shuffled(n_dev, 1)))]
    near += [lax.ppermute(own[g], "dev", shuffled(n_dev, 1)) for g in range(1, groups)]
    across = lax.ppermute(turned_bd, "col", shuffled(n_col, 2))
    beside = lax.ppermute(turned_bd, "col", shuffled(n_col, 1))
    diagonal = lax.ppermute(across, "col", shuffled(n_col, 1))
    whole_bd, token = gathered((turned_bd, beside, across, diagonal))

    core, chip = col % 2, col // 2

    def joined(keeper, pair):
        away = [(i, i ^ 1) for i in range(n_col) if i % 2 != keeper]
        across_chips = [(i, i ^ 2) for i in range(n_col) if i % 2 == keeper]
        both = jnp.stack(pair)
        both = both + lax.ppermute(both, "col", away)
        give = lax.dynamic_index_in_dim(both, 1 - chip, 0, keepdims=False)
        keep = lax.dynamic_index_in_dim(both, chip, 0, keepdims=False)
        return keep + lax.ppermute(give, "col", across_chips)

    totals = [jnp.zeros((b_count * ROWS, pairs), F32)] * groups
    ready = []

    def send(g, *gates):
        mine, other, *_ = lax.optimization_barrier((own[g], near[g], *gates))
        for i, (c0, c1) in enumerate(spans[g]):
            held = jnp.concatenate([x[c0 * ROWS:c1 * ROWS] for x in (mine, other)], axis=0)
            far = lax.ppermute(held, "dev", INNER)
            ready.append((g, i, c0, held, far, lax.ppermute(far, "dev", TO_END)))

    def work(g):
        for h, i, c0, *parts in ready:
            if h == g:
                totals[g] = block(i == 0, where, parts, whole_bd, amplitudes, c0, totals[g])
        return totals[g]

    send(0)
    send(1)
    send(2, token)
    send(3, work(0))
    for g in range(1, groups):
        work(g)
    lower = joined(0, totals[:2])
    third, lower = lax.optimization_barrier((totals[2], lower))
    away = [(i, i ^ 1) for i in range(n_col) if i % 2 == 0]
    third = third + lax.ppermute(third, "col", away)
    fourth, third = lax.optimization_barrier((totals[3], third))
    fourth = fourth + lax.ppermute(fourth, "col", away)
    keep, give = jnp.where(chip == 0, third, fourth), jnp.where(chip == 0, fourth, third)
    upper = keep + lax.ppermute(give, "col", [(i, i ^ 2) for i in range(n_col) if i % 2 == 1])
    mine = jnp.where(core == 0, lower, upper)
    mine = mine.reshape(n_dev, b_count // n_dev * ROWS, pairs)
    out = lax.dynamic_index_in_dim(mine, dev, 0, keepdims=False)
    for mask in (3, 2, 1):
        give = lax.dynamic_index_in_dim(mine, dev ^ mask, 0, keepdims=False)
        out = out + lax.ppermute(give, "dev", shuffled(n_dev, mask))
    return out.reshape(b_count // n_dev, ROWS, pairs).transpose(1, 0, 2)


def solution(mesh):
    n_dev, n_col = mesh.shape["dev"], mesh.shape["col"]
    placed = (
        P(("frag", "dev"), None, "col"),
        P(("frag", "col"), None, "dev"),
        P(("frag", "col"), "dev", None),
    )

    def local(factor_ac, factor_bd, amplitudes):
        depth, a_count, c_count = factor_ac.shape
        _, b_count, width = factor_bd.shape
        fits = n_dev == 4 and n_col == 4 and width == 128 and depth % 128 == 0
        fits = fits and a_count == ROWS * n_col and b_count % 16 == 0 and c_count % 128 == 0
        if fits:
            return laddered(n_dev, n_col, factor_ac, factor_bd, amplitudes)
        return plain(factor_ac, factor_bd, amplitudes)

    return jax.shard_map(
        local,
        mesh=mesh,
        in_specs=placed,
        out_specs=P(("frag", "col"), "dev", None),
        check_vma=False,
    )
```
